32 devices in a mesh: space: 8 (over z, core), tm: 4 (over y, x).
Axes of the slice: x: 2, y: 2, z: 4, core: 2. Of those that a mesh axis runs over, the one named last changes fastest.
Arguments:
- snapshots: bfloat16 [32768, 512], P('space', 'tm'), may hold values from -6 to 6
- stencil_starts: int32 [512], P('tm'), may hold values from 0 to 508, as said below
- stencil_widths: int32 [512], P('tm'), may hold values from 4 to 40, as said below
- stencil_coeffs: bfloat16 [512, 40], P('tm'), may hold values from -2 to 2
- panels: bfloat16 [512, 256], P('tm'), may hold values from -0.25 to 0.25
Outputs:
- gram: float32 [512, 512], P(('tm', 'space'))
- modes: bfloat16 [32768, 256], P(('space', 'tm'))
The draws below stay inside these ranges and needn't reach their ends.
Inputs may be any that keep to these rules, and one draw needn't show every extreme that they name: `stencil_starts`: uniform time u's stencil starts inside its own time block, snapshots from (u // 128) * 128 to that plus 128 - 1, and ends before snapshot 512. `stencil_widths`: some stencil has width 40 and some has width 4.
All inputs are finite; a program needn't handle non-finite values.
Results may differ from the reference program's by a relative error of at most 0.0049.
Values may be sent and summed in bfloat16 or wider, within the bound.
A program may use at most 64 MiB of HBM per device.

```python
import jax
import jax.numpy as jnp
from jax import lax

U_DEV = 128
WMAX = 40
NMODE = 256
NU = 512
ROWS = 32768


def stencil_pair(key):
    blocks = NU // U_DEV
    block_high = jax.random.randint(jax.random.fold_in(key, 11), (blocks,), 8, WMAX + 1)
    high = jnp.repeat(block_high, U_DEV)
    raw = jax.random.randint(jax.random.fold_in(key, 12), (NU,), 0, 1048576)
    widths = 4 + raw % (high - 3)
    widths = widths.at[0].set(WMAX).at[1].set(4)
    offsets = jax.random.randint(jax.random.fold_in(key, 13), (NU,), 0, U_DEV)
    starts = jnp.arange(NU, dtype=jnp.int32) // U_DEV * U_DEV + offsets
    starts = jnp.minimum(starts, NU - widths)
    return (starts.astype(jnp.int32), widths.astype(jnp.int32))


def draw_stencil_starts(key, part):
    return stencil_pair(key)[0]


def draw_stencil_widths(key, part):
    return stencil_pair(key)[1]


def strengthened(drawn, key, source, target, shards_of, factor):
    def block_of(dim):
        return (jnp.arange(drawn.shape[dim]) // (drawn.shape[dim] // shards_of)).reshape((-1,) + (1,) * (drawn.ndim - 1 - dim))

    near = jax.random.permutation(key, shards_of)[block_of(target)]
    other_side = (block_of(target) + shards_of // 2) % shards_of
    return jnp.where((block_of(source) == near) | (block_of(source) == other_side), factor * drawn, drawn)


def block_scale(stream_key, dims, shards, low, largest):
    gain, own = 1.0, jax.random.fold_in(stream_key, 6)
    for axis_at, shards_of in shards:
        heights = jnp.exp(jax.random.uniform(jax.random.fold_in(own, axis_at), (shards_of,), jnp.float32, low / len(shards), largest / len(shards)))
        gain = gain * jnp.repeat(heights, dims[axis_at] // shards_of).reshape([-1 if axis == axis_at else 1 for axis in range(len(dims))])
    return gain


def bell_draw(own_key, dims, width, limit, pieces=(), kind=jnp.bfloat16):
    drawn = width * jax.random.normal(own_key, dims, jnp.float32)
    if pieces:
        drawn = drawn * block_scale(own_key, dims, pieces, -0.22, 0.18)
    return jnp.clip(drawn, -limit, limit).astype(kind)


def bell_draw_with(own_key, extent, spread, most, shards, heavy, held_as=jnp.bfloat16):
    result = spread * jax.random.normal(own_key, extent, jnp.float32)
    if shards:
        result = result * block_scale(own_key, extent, shards, -0.22, 0.18)
    return jnp.clip(strengthened(result, jax.random.fold_in(own_key, 3), *heavy), -most, most).astype(held_as)


def setup_inputs(seed: int = 0) -> dict:
    keys = jax.random.split(jax.random.key(seed), 6)
    return {
        "snapshots": bell_draw_with(keys[0], (ROWS, NU), 1.0, 6.0, ((0, 8), (1, 4)), (0, 1, 8, 2.0)),
        "stencil_starts": draw_stencil_starts(jax.random.fold_in(keys[5], 71), 0),
        "stencil_widths": draw_stencil_widths(jax.random.fold_in(keys[5], 71), 0),
        "stencil_coeffs": bell_draw(keys[3], (NU, WMAX), 0.3, 2.0, ((0, 4),)),
        "panels": bell_draw(keys[4], (NU, NMODE), NU ** -0.5, 0.25, ((0, 4),)),
    }


def stencil_matrix(stencil_starts, stencil_widths, stencil_coeffs):
    position = jnp.arange(NU, dtype=jnp.int32)[:, None]
    offset = position - stencil_starts[None, :]
    weights = jnp.zeros((NU, NU), jnp.float32)
    for step in range(WMAX):
        picked = (offset == step) & (step < stencil_widths[None, :])
        weights = weights + jnp.where(picked, stencil_coeffs[:, step].astype(jnp.float32)[None, :], 0.0)
    return weights.astype(jnp.bfloat16)


def reference(snapshots, stencil_starts, stencil_widths, stencil_coeffs, panels):
    weights = stencil_matrix(stencil_starts, stencil_widths, stencil_coeffs)
    resampled = jnp.dot(snapshots, weights, preferred_element_type=jnp.float32).astype(jnp.bfloat16)
    gram = lax.dot_general(resampled, resampled, (((0,), (0,)), ((), ())), preferred_element_type=jnp.float32)
    gram = gram * (1.0 / ROWS)
    modes = jnp.dot(resampled, panels, preferred_element_type=jnp.float32).astype(jnp.bfloat16)
    return gram, modes
```

```python
import functools

import jax
import jax.numpy as jnp
from jax import lax
from jax.experimental import pallas as pl
from jax.experimental.pallas import tpu as pltpu
from jax.sharding import PartitionSpec as P

F32 = jnp.float32
BF16 = jnp.bfloat16
CORES = 2


def shifted(value, axis, steps):
    count = lax.axis_size(axis)
    initial, last = (max(0, -steps), min(count, count - steps))
    return lax.ppermute(value, axis, [(source, source + steps) for source in range(initial, last)])


def on_device(snapshots, stencil_starts, stencil_widths, stencil_coeffs, panels):
    rows, block = snapshots.shape
    width_max = stencil_coeffs.shape[1]
    rim = shifted(snapshots[:, : width_max - 1], "tm", -1)
    extended = jnp.concatenate([snapshots, rim], axis=1)
    offsets = stencil_starts - lax.axis_index("tm") * block
    position = jnp.arange(block + width_max - 1, dtype=jnp.int32)[:, None]
    relative = position - offsets[None, :]
    steps = jnp.arange(width_max, dtype=jnp.int32)[:, None, None]
    picked = (relative[None, :, :] == steps) & (steps < stencil_widths[None, None, :])
    coeff_table = stencil_coeffs.T[:, None, :].astype(F32)
    weights = jnp.sum(jnp.where(picked, coeff_table, 0.0), axis=0).astype(BF16)
    resampled = jnp.dot(extended, weights, preferred_element_type=F32).astype(BF16)
    scale = 1.0 / (rows * lax.axis_size("space"))
    share = rows // lax.axis_size("tm")
    whole = lax.all_gather(resampled, "tm", axis=1, tiled=True)
    partial_value = lax.dot_general(
        resampled, whole, (((0,), (0,)), ((), ())), preferred_element_type=F32
    )
    every_panel = lax.all_gather(panels, "tm", axis=0, tiled=True)
    mine = lax.dynamic_slice_in_dim(whole, lax.axis_index("tm") * share, share, 0)
    modes = jnp.dot(mine, every_panel, preferred_element_type=F32).astype(BF16)
    partial_value = partial_value * scale
    gram = lax.psum_scatter(partial_value, "space", scatter_dimension=0, tiled=True)
    return (gram, modes)


def spread(packed, width_max, block):
    table = packed.astype(F32)
    rows = table.shape[0]
    moved = table[width_max : width_max + 1, :].astype(jnp.int32)
    index = lax.broadcasted_iota(jnp.int32, table.shape, 0)
    value = jnp.where(index < width_max, table, 0.0)
    step = 1
    while step < block:
        chosen = (moved & step) != 0
        if step < 8:
            other = pltpu.roll(value, step, 0)
        else:
            empty = jnp.zeros((step, block), F32)
            other = jnp.concatenate([empty, value], axis=0)
            value = jnp.concatenate([value, empty], axis=0)
        value = jnp.where(jnp.broadcast_to(chosen, value.shape), other, value)
        step *= 2
    return value


def kernel(
    nsp, ntm, chunks, width_max,
    snap, starts, widths, coeffs, panels,
    gram_out, modes_out,
    packed, weights, gathered, resampled, acc, pair_in, mine32, tm_out, tm_in, z_out, z_in, panel_all, modes_buf,
    local_sem, pack_send, pack_recv, row_send, row_recv, panel_send, panel_recv,
    pair_send, pair_recv, tm_send, tm_recv, z_send, z_recv,
):
    space = lax.axis_index("space")
    t = lax.axis_index("tm")
    zz, core = space // CORES, space % CORES
    nz = nsp // CORES
    block = snap.shape[1]
    share = snap.shape[0] // ntm
    piece = share // chunks
    nu = block * ntm

    def at(space_id, tm_id):
        return dict(device_id=(space_id, tm_id), device_id_type=pl.DeviceIdType.MESH)

    tm_peers = [lax.rem(t + d, ntm) for d in range(1, ntm)]
    z_peers = [lax.rem(zz + d, nz) * CORES + core for d in range(1, nz)]
    partner = zz * CORES + (1 - core)

    barrier = pltpu.get_barrier_semaphore()
    for peer in z_peers:
        pl.semaphore_signal(barrier, inc=1, **at(peer, t))
    for peer in tm_peers:
        pl.semaphore_signal(barrier, inc=1, **at(space, peer))
    pl.semaphore_signal(barrier, inc=1, **at(partner, t))

    own_rows = pltpu.make_async_copy(
        snap.at[pl.ds(t * share, share), :],
        gathered.at[:, pl.ds(pl.multiple_of(t * block, block), block)],
        local_sem.at[0],
    )
    own_rows.start()
    own_panels = pltpu.make_async_copy(
        panels, panel_all.at[pl.ds(pl.multiple_of(t * block, block), block), :], local_sem.at[1]
    )
    own_panels.start()

    prow = packed.shape[1]
    unit = (
        lax.broadcasted_iota(jnp.int32, (prow, width_max), 0)
        == lax.broadcasted_iota(jnp.int32, (prow, width_max), 1)
    ).astype(F32).astype(BF16)
    turned = lax.dot_general(unit, coeffs[...], (((1,), (1,)), ((), ())), preferred_element_type=F32)
    index = lax.broadcasted_iota(jnp.int32, turned.shape, 0)
    offset = (starts[...] - t * block).astype(F32)
    table = jnp.where(index < jnp.broadcast_to(widths[...], turned.shape), turned, 0.0)
    table = jnp.where(index == width_max, jnp.broadcast_to(offset, turned.shape), table)
    packed[t] = table.astype(BF16)

    pl.semaphore_wait(barrier, len(z_peers) + len(tm_peers) + 1)

    sends = []
    for i, peer in enumerate(tm_peers):
        sends.append(pltpu.make_async_remote_copy(
            src_ref=packed.at[t], dst_ref=packed.at[t],
            send_sem=pack_send.at[i], recv_sem=pack_recv.at[i], **at(space, peer)))
        sends[-1].start()
    for c in range(chunks):
        for i, peer in enumerate(tm_peers):
            sends.append(pltpu.make_async_remote_copy(
                src_ref=snap.at[pl.ds(pl.multiple_of(peer * share + c * piece, piece), piece), :],
                dst_ref=gathered.at[pl.ds(c * piece, piece), pl.ds(pl.multiple_of(t * block, block), block)],
                send_sem=row_send.at[c, i], recv_sem=row_recv.at[c, i], **at(space, peer)))
            sends[-1].start()
    for i, peer in enumerate(tm_peers):
        sends.append(pltpu.make_async_remote_copy(
            src_ref=panels, dst_ref=panel_all.at[pl.ds(pl.multiple_of(t * block, block), block), :],
            send_sem=panel_send.at[i], recv_sem=panel_recv.at[i], **at(space, peer)))
        sends[-1].start()

    weights[...] = jnp.zeros_like(weights)
    acc[...] = jnp.zeros_like(acc)

    def arrival(dst, sem):
        return pltpu.make_async_remote_copy(
            src_ref=dst, dst_ref=dst, send_sem=sem, recv_sem=sem, **at(space, tm_peers[0]))

    def origin(i):
        return lax.rem(t + ntm - (i + 1), ntm)

    for i in range(ntm - 1):
        arrival(packed.at[origin(i)], pack_recv.at[i]).wait_recv()
    for b in range(ntm):
        value = spread(packed[b], width_max, block).astype(BF16)
        height = min(value.shape[0], nu - b * block)
        weights[b * block : b * block + height, b * block : (b + 1) * block] = value[:height]

    own_rows.wait()
    span = CORES * block

    def chunk_step(c, carry):
        at_rows = pl.ds(pl.multiple_of(c * piece, piece), piece)
        for i in range(ntm - 1):
            arrival(
                gathered.at[at_rows, pl.ds(pl.multiple_of(origin(i) * block, block), block)], row_recv.at[c, i]
            ).wait_recv()
        for first in range(0, nu, span):
            last = min(first + 2 * span, nu)
            part = jnp.dot(
                gathered[at_rows, first:last], weights[first:last, first : first + span],
                preferred_element_type=F32,
            )
            resampled[at_rows, first : first + span] = part.astype(BF16)
        rows = resampled[at_rows, :]
        acc[...] += lax.dot_general(
            rows, rows, (((0,), (0,)), ((), ())), preferred_element_type=F32
        ).reshape(acc.shape)
        return carry

    lax.fori_loop(0, chunks, chunk_step, 0)

    pair = pltpu.make_async_remote_copy(
        src_ref=acc.at[:, 1 - core], dst_ref=pair_in,
        send_sem=pair_send, recv_sem=pair_recv, **at(partner, t))
    pair.start()

    own_panels.wait()
    for i in range(ntm - 1):
        arrival(panel_all.at[pl.ds(pl.multiple_of(origin(i) * block, block), block), :], panel_recv.at[i]).wait_recv()

    def modes_step(c, carry):
        at_rows = pl.ds(pl.multiple_of(c * piece, piece), piece)
        modes_buf[at_rows, :] = jnp.dot(
            resampled[at_rows, :], panel_all[...], preferred_element_type=F32).astype(BF16)
        return carry

    pair.wait_recv()
    summed = acc[:, pl.ds(core, 1)].reshape(pair_in.shape) + pair_in[...]
    summed = summed.reshape(mine32.shape)
    mine32[...] = summed
    tm_out[...] = summed.astype(BF16)
    for i, peer in enumerate(tm_peers):
        sends.append(pltpu.make_async_remote_copy(
            src_ref=tm_out.at[peer], dst_ref=tm_in.at[i],
            send_sem=tm_send.at[i], recv_sem=tm_recv.at[i], **at(space, peer)))
        sends[-1].start()
    lax.fori_loop(0, chunks, modes_step, 0)
    modes_copy = pltpu.make_async_copy(modes_buf, modes_out, local_sem.at[2])
    modes_copy.start()
    total = mine32[t]
    for i in range(ntm - 1):
        arrival(tm_in.at[i], tm_recv.at[i]).wait_recv()
        total = total + tm_in[i].astype(F32)
    mine32[t] = total
    z_out[...] = total.astype(BF16)
    for i, peer in enumerate(z_peers):
        sends.append(pltpu.make_async_remote_copy(
            src_ref=z_out.at[lax.rem(zz + i + 1, nz)], dst_ref=z_in.at[i],
            send_sem=z_send.at[i], recv_sem=z_recv.at[i], **at(peer, t)))
        sends[-1].start()
    final = mine32[t, zz]
    for i in range(nz - 1):
        arrival(z_in.at[i], z_recv.at[i]).wait_recv()
        final = final + z_in[i].astype(F32)
    gram_out[...] = final * (1.0 / (snap.shape[0] * nsp))

    pair.wait_send()
    for copy in sends:
        copy.wait_send()
    modes_copy.wait()


def fused(nsp, ntm, snapshots, stencil_starts, stencil_widths, stencil_coeffs, panels):
    rows, block = snapshots.shape
    width_max = stencil_coeffs.shape[1]
    nmode = panels.shape[1]
    nu, share, nz = block * ntm, rows // ntm, nsp // CORES
    own = nu // (ntm * nsp)
    chunks = 4
    prow = -(-(width_max + 1) // 16) * 16
    vmem = pl.BlockSpec(memory_space=pltpu.VMEM)
    hbm = pl.BlockSpec(memory_space=pl.ANY)
    dma = pltpu.SemaphoreType.DMA
    call = pl.pallas_call(
        functools.partial(kernel, nsp, ntm, chunks, width_max),
        out_shape=(
            jax.ShapeDtypeStruct((own, nu), F32),
            jax.ShapeDtypeStruct((share, nmode), BF16),
        ),
        in_specs=[hbm, vmem, vmem, vmem, vmem],
        out_specs=(vmem, hbm),
        scratch_shapes=[
            pltpu.VMEM((ntm, prow, block), BF16),
            pltpu.VMEM((nu, nu), BF16),
            pltpu.VMEM((share, nu), BF16),
            pltpu.VMEM((share, nu), BF16),
            pltpu.VMEM((ntm * nz, CORES, own, nu), F32),
            pltpu.VMEM((ntm * nz, own, nu), F32),
            pltpu.VMEM((ntm, nz, own, nu), F32),
            pltpu.VMEM((ntm, nz, own, nu), BF16),
            pltpu.VMEM((ntm - 1, nz, own, nu), BF16),
            pltpu.VMEM((nz, own, nu), BF16),
            pltpu.VMEM((nz - 1, own, nu), BF16),
            pltpu.VMEM((nu, nmode), BF16),
            pltpu.VMEM((share, nmode), BF16),
            dma((3,)),
            dma((ntm - 1,)),
            dma((ntm - 1,)),
            dma((chunks, ntm - 1)),
            dma((chunks, ntm - 1)),
            dma((ntm - 1,)),
            dma((ntm - 1,)),
            dma,
            dma,
            dma((ntm - 1,)),
            dma((ntm - 1,)),
            dma((nz - 1,)),
            dma((nz - 1,)),
        ],
        compiler_params=pltpu.CompilerParams(
            collective_id=0, has_side_effects=True, vmem_limit_bytes=48 * 1024 * 1024
        ),
    )
    return call(
        snapshots, stencil_starts.reshape(1, block), stencil_widths.reshape(1, block), stencil_coeffs, panels
    )


def solution(mesh):
    nsp, ntm = mesh.shape["space"], mesh.shape["tm"]

    def body(snapshots, stencil_starts, stencil_widths, stencil_coeffs, panels):
        rows, block = snapshots.shape
        own = block // nsp
        fits = block == 128 and own % 16 == 0 and nsp % CORES == 0 and ntm % 2 == 0 and rows % (64 * ntm) == 0
        if fits and 4 * (block * ntm) ** 2 <= 4 * 1024 * 1024:
            return fused(nsp, ntm, snapshots, stencil_starts, stencil_widths, stencil_coeffs, panels)
        return on_device(snapshots, stencil_starts, stencil_widths, stencil_coeffs, panels)

    return jax.shard_map(
        body,
        mesh=mesh,
        in_specs=(P("space", "tm"), P("tm"), P("tm"), P("tm", None), P("tm", None)),
        out_specs=(P(("tm", "space"), None), P(("space", "tm"), None)),
        check_vma=False,
    )
```

```python
import functools

import jax
import jax.numpy as jnp
from jax import lax
from jax.experimental import pallas as pl
from jax.experimental.pallas import tpu as pltpu
from jax.sharding import PartitionSpec as P

F32 = jnp.float32
BF16 = jnp.bfloat16
CORES = 2
CHUNKS = 8


def shifted(value, axis, steps):
    count = lax.axis_size(axis)
    initial, last = (max(0, -steps), min(count, count - steps))
    return lax.ppermute(value, axis, [(source, source + steps) for source in range(initial, last)])


def on_device(snapshots, stencil_starts, stencil_widths, stencil_coeffs, panels):
    rows, block = snapshots.shape
    width_max = stencil_coeffs.shape[1]
    rim = shifted(snapshots[:, : width_max - 1], "tm", -1)
    extended = jnp.concatenate([snapshots, rim], axis=1)
    offsets = stencil_starts - lax.axis_index("tm") * block
    position = jnp.arange(block + width_max - 1, dtype=jnp.int32)[:, None]
    relative = position - offsets[None, :]
    steps = jnp.arange(width_max, dtype=jnp.int32)[:, None, None]
    picked = (relative[None, :, :] == steps) & (steps < stencil_widths[None, None, :])
    coeff_table = stencil_coeffs.T[:, None, :].astype(F32)
    weights = jnp.sum(jnp.where(picked, coeff_table, 0.0), axis=0).astype(BF16)
    resampled = jnp.dot(extended, weights, preferred_element_type=F32).astype(BF16)
    scale = 1.0 / (rows * lax.axis_size("space"))
    share = rows // lax.axis_size("tm")
    whole = lax.all_gather(resampled, "tm", axis=1, tiled=True)
    partial_value = lax.dot_general(
        resampled, whole, (((0,), (0,)), ((), ())), preferred_element_type=F32
    )
    every_panel = lax.all_gather(panels, "tm", axis=0, tiled=True)
    mine = lax.dynamic_slice_in_dim(whole, lax.axis_index("tm") * share, share, 0)
    modes = jnp.dot(mine, every_panel, preferred_element_type=F32).astype(BF16)
    partial_value = partial_value * scale
    gram = lax.psum_scatter(partial_value, "space", scatter_dimension=0, tiled=True)
    return (gram, modes)


def spread(packed, width_max, block):
    table = packed.astype(F32)
    rows = table.shape[0]
    moved = table[width_max : width_max + 1, :].astype(jnp.int32)
    index = lax.broadcasted_iota(jnp.int32, table.shape, 0)
    value = jnp.where(index < width_max, table, 0.0)
    step = 1
    while step < block:
        chosen = (moved & step) != 0
        if step < 8:
            other = pltpu.roll(value, step, 0)
        else:
            empty = jnp.zeros((step, block), F32)
            other = jnp.concatenate([empty, value], axis=0)
            value = jnp.concatenate([value, empty], axis=0)
        value = jnp.where(jnp.broadcast_to(chosen, value.shape), other, value)
        step *= 2
    return value


def kernel(
    nsp, ntm, chunks, halves, width_max,
    snap, starts_in, widths_in, coeffs_in, panels,
    gram_out, modes_out,
    starts, widths, coeffs,
    packed, weights, gathered, resampled, acc, pair_in, mine32, tm_out, tm_in, z_out, z_in, panel_all,
    local_sem, pack_send, pack_recv, row_send, row_recv, panel_send, panel_recv,
    pair_send, pair_recv, tm_send, tm_recv, z_send, z_recv,
):
    space = lax.axis_index("space")
    t = lax.axis_index("tm")
    zz, core = space // CORES, space % CORES
    nz = nsp // CORES
    block = snap.shape[1]
    share = snap.shape[0] // ntm
    piece = share // chunks
    nu = block * ntm
    wide = nu // halves

    def at(space_id, tm_id):
        return dict(device_id=(space_id, tm_id), device_id_type=pl.DeviceIdType.MESH)

    tm_peers = [lax.rem(t + d, ntm) for d in range(1, ntm)]
    z_peers = [lax.rem(zz + d, nz) * CORES + core for d in range(1, nz)]
    partner = zz * CORES + (1 - core)

    barrier = pltpu.get_barrier_semaphore()
    for peer in z_peers:
        pl.semaphore_signal(barrier, inc=1, **at(peer, t))
    for peer in tm_peers:
        pl.semaphore_signal(barrier, inc=1, **at(space, peer))
    pl.semaphore_signal(barrier, inc=1, **at(partner, t))

    columns = pl.ds(pl.multiple_of(t * block, block), block)
    small = [
        pltpu.make_async_copy(source, target, local_sem.at[i])
        for i, (source, target) in enumerate(
            [(starts_in, starts), (widths_in, widths), (coeffs_in, coeffs)]
        )
    ]
    own_rows = pltpu.make_async_copy(
        snap.at[pl.ds(pl.multiple_of(t * share, share), share), :], gathered.at[:, columns], local_sem.at[3]
    )
    own_panels = pltpu.make_async_copy(panels, panel_all.at[columns, :], local_sem.at[4])
    for copy in small:
        copy.start()
    own_rows.start()
    own_panels.start()

    for copy in small:
        copy.wait()
    prow = packed.shape[1]
    turned = jnp.concatenate(
        [coeffs[...].astype(F32), jnp.zeros((prow - width_max, block), F32)], axis=0
    )
    index = lax.broadcasted_iota(jnp.int32, turned.shape, 0)
    offset = (starts[...] - t * block).astype(F32)
    table = jnp.where(index < jnp.broadcast_to(widths[...], turned.shape), turned, 0.0)
    table = jnp.where(index == width_max, jnp.broadcast_to(offset, turned.shape), table)
    packed[t] = table.astype(BF16)

    pl.semaphore_wait(barrier, len(z_peers) + len(tm_peers) + 1)

    sends = []

    def send(src, dst, send_sem, recv_sem, space_id, tm_id):
        copy = pltpu.make_async_remote_copy(
            src_ref=src, dst_ref=dst, send_sem=send_sem, recv_sem=recv_sem, **at(space_id, tm_id))
        copy.start()
        sends.append(copy)

    for i, peer in enumerate(tm_peers):
        send(packed.at[t], packed.at[t], pack_send.at[i], pack_recv.at[i], space, peer)
    for c in range(chunks):
        for i, peer in enumerate(tm_peers):
            send(
                snap.at[pl.ds(pl.multiple_of(peer * share + c * piece, piece), piece), :],
                gathered.at[pl.ds(c * piece, piece), columns],
                row_send.at[c, i], row_recv.at[c, i], space, peer)
    for i, peer in enumerate(tm_peers):
        send(panels, panel_all.at[columns, :], panel_send.at[i], panel_recv.at[i], space, peer)

    weights[...] = jnp.zeros_like(weights)
    acc[...] = jnp.zeros_like(acc)

    def arrived(dst, sem):
        pltpu.make_async_remote_copy(
            src_ref=dst, dst_ref=dst, send_sem=sem, recv_sem=sem, **at(space, tm_peers[0])
        ).wait_recv()

    origins = [lax.rem(t + ntm - d, ntm) for d in range(1, ntm)]

    for i, origin in enumerate(origins):
        arrived(packed.at[origin], pack_recv.at[i])
    for b in range(ntm):
        value = spread(packed[b], width_max, block).astype(BF16)
        height = min(value.shape[0], nu - b * block)
        weights[b * block : b * block + height, b * block : (b + 1) * block] = value[:height]

    own_rows.wait()
    span = CORES * block

    def resample(c):
        at_rows = pl.ds(pl.multiple_of(c * piece, piece), piece)
        for i, origin in enumerate(origins):
            arrived(
                gathered.at[at_rows, pl.ds(pl.multiple_of(origin * block, block), block)], row_recv.at[c, i]
            )
        for first in range(0, nu, span):
            last = min(first + 2 * span, nu)
            part = jnp.dot(
                gathered[at_rows, first:last], weights[first:last, first : first + span],
                preferred_element_type=F32,
            )
            resampled[at_rows, first : first + span] = part.astype(BF16)
        return resampled[at_rows, :]

    def product(left, right):
        value = lax.dot_general(left, right, (((0,), (0,)), ((), ())), preferred_element_type=F32)
        return value.reshape(acc.shape[:3] + (right.shape[1],))

    def chunk_step(c, carry):
        rows = resample(c)
        acc[...] += product(rows, rows)
        return carry

    lax.fori_loop(0, chunks - 1, chunk_step, 0)
    parts = [slice(h * wide, (h + 1) * wide) for h in range(halves)]
    rows = resample(chunks - 1)
    for h, part in enumerate(parts):
        acc[:, :, :, part] += product(rows, rows[:, part])
        send(acc.at[:, 1 - core, :, part], pair_in.at[:, :, part], pair_send.at[h], pair_recv.at[h], partner, t)

    for h, part in enumerate(parts):
        arrived(pair_in.at[:, :, part], pair_recv.at[h])
        summed = acc[:, pl.ds(core, 1), :, part].reshape(pair_in.shape[:2] + (wide,)) + pair_in[:, :, part]
        summed = summed.reshape(mine32.shape[:3] + (wide,))
        mine32[:, :, :, part] = summed
        tm_out[:, :, :, part] = summed.astype(BF16)
        for i, peer in enumerate(tm_peers):
            send(
                tm_out.at[peer, :, :, part], tm_in.at[i, :, :, part],
                tm_send.at[h, i], tm_recv.at[h, i], space, peer)

    own_panels.wait()
    for i, origin in enumerate(origins):
        arrived(panel_all.at[pl.ds(pl.multiple_of(origin * block, block), block), :], panel_recv.at[i])

    def modes_step(c, carry):
        at_rows = pl.ds(pl.multiple_of(c * piece, piece), piece)
        modes_out[at_rows, :] = jnp.dot(
            resampled[at_rows, :], panel_all[...], preferred_element_type=F32).astype(BF16)
        return carry

    lax.fori_loop(0, chunks, modes_step, 0)

    for h, part in enumerate(parts):
        total = mine32[pl.ds(t, 1), :, :, part].reshape(z_out.shape[:2] + (wide,))
        for i in range(ntm - 1):
            arrived(tm_in.at[i, :, :, part], tm_recv.at[h, i])
            total = total + tm_in[i, :, :, part].astype(F32)
        mine32[pl.ds(t, 1), :, :, part] = total[None]
        z_out[:, :, part] = total.astype(BF16)
        for i, peer in enumerate(z_peers):
            send(
                z_out.at[lax.rem(zz + i + 1, nz), :, part], z_in.at[i, :, part],
                z_send.at[h, i], z_recv.at[h, i], peer, t)
    for h, part in enumerate(parts):
        final = mine32[pl.ds(t, 1), pl.ds(zz, 1), :, part].reshape(gram_out.shape[0], wide)
        for i in range(nz - 1):
            arrived(z_in.at[i, :, part], z_recv.at[h, i])
            final = final + z_in[i, :, part].astype(F32)
        gram_out[:, part] = final * (1.0 / (snap.shape[0] * nsp))

    for copy in sends:
        copy.wait_send()


def fused(nsp, ntm, snapshots, stencil_starts, stencil_widths, stencil_coeffs, panels):
    rows, block = snapshots.shape
    width_max = stencil_coeffs.shape[1]
    nmode = panels.shape[1]
    nu, share, nz = block * ntm, rows // ntm, nsp // CORES
    own = nu // (ntm * nsp)
    chunks, halves = CHUNKS, 2
    prow = -(-(width_max + 1) // 16) * 16
    vmem = pl.BlockSpec(memory_space=pltpu.VMEM)
    hbm = pl.BlockSpec(memory_space=pltpu.HBM)
    dma = pltpu.SemaphoreType.DMA
    call = pl.pallas_call(
        functools.partial(kernel, nsp, ntm, chunks, halves, width_max),
        out_shape=(
            jax.ShapeDtypeStruct((own, nu), F32),
            jax.ShapeDtypeStruct((share, nmode), BF16),
        ),
        in_specs=[hbm, hbm, hbm, hbm, hbm],
        out_specs=(vmem, vmem),
        scratch_shapes=[
            pltpu.VMEM((1, block), jnp.int32),
            pltpu.VMEM((1, block), jnp.int32),
            pltpu.VMEM((width_max, block), BF16),
            pltpu.VMEM((ntm, prow, block), BF16),
            pltpu.VMEM((nu, nu), BF16),
            pltpu.VMEM((share, nu), BF16),
            pltpu.VMEM((share, nu), BF16),
            pltpu.VMEM((ntm * nz, CORES, own, nu), F32),
            pltpu.VMEM((ntm * nz, own, nu), F32),
            pltpu.VMEM((ntm, nz, own, nu), F32),
            pltpu.VMEM((ntm, nz, own, nu), BF16),
            pltpu.VMEM((ntm - 1, nz, own, nu), BF16),
            pltpu.VMEM((nz, own, nu), BF16),
            pltpu.VMEM((nz - 1, own, nu), BF16),
            pltpu.VMEM((nu, nmode), BF16),
            dma((5,)),
            dma((ntm - 1,)),
            dma((ntm - 1,)),
            dma((chunks, ntm - 1)),
            dma((chunks, ntm - 1)),
            dma((ntm - 1,)),
            dma((ntm - 1,)),
            dma((halves,)),
            dma((halves,)),
            dma((halves, ntm - 1)),
            dma((halves, ntm - 1)),
            dma((halves, nz - 1)),
            dma((halves, nz - 1)),
        ],
        compiler_params=pltpu.CompilerParams(
            collective_id=0, has_side_effects=True, vmem_limit_bytes=48 * 1024 * 1024
        ),
    )
    operands = (
        snapshots, stencil_starts.reshape(1, block), stencil_widths.reshape(1, block), stencil_coeffs.T, panels
    )
    return call(*(pltpu.with_memory_space_constraint(operand, pltpu.HBM) for operand in operands))


def solution(mesh):
    nsp, ntm = mesh.shape["space"], mesh.shape["tm"]

    def body(snapshots, stencil_starts, stencil_widths, stencil_coeffs, panels):
        rows, block = snapshots.shape
        own = block // nsp
        fits = block == 128 and own % 16 == 0 and nsp % CORES == 0 and ntm % 2 == 0 and rows % (64 * ntm) == 0
        if fits and 4 * (block * ntm) ** 2 <= 4 * 1024 * 1024:
            return fused(nsp, ntm, snapshots, stencil_starts, stencil_widths, stencil_coeffs, panels)
        return on_device(snapshots, stencil_starts, stencil_widths, stencil_coeffs, panels)

    return jax.shard_map(
        body,
        mesh=mesh,
        in_specs=(P("space", "tm"), P("tm"), P("tm"), P("tm", None), P("tm", None)),
        out_specs=(P(("tm", "space"), None), P(("space", "tm"), None)),
        check_vma=False,
    )
```

```python
import functools

import jax
import jax.numpy as jnp
from jax import lax
from jax.experimental import pallas as pl
from jax.experimental.pallas import tpu as pltpu
from jax.sharding import PartitionSpec as P

F32 = jnp.float32
BF16 = jnp.bfloat16
CORES = 2
CHUNKS = 8


def shifted(value, axis, steps):
    count = lax.axis_size(axis)
    initial, last = (max(0, -steps), min(count, count - steps))
    return lax.ppermute(value, axis, [(source, source + steps) for source in range(initial, last)])


def on_device(snapshots, stencil_starts, stencil_widths, stencil_coeffs, panels):
    rows, block = snapshots.shape
    width_max = stencil_coeffs.shape[1]
    rim = shifted(snapshots[:, : width_max - 1], "tm", -1)
    extended = jnp.concatenate([snapshots, rim], axis=1)
    offsets = stencil_starts - lax.axis_index("tm") * block
    position = jnp.arange(block + width_max - 1, dtype=jnp.int32)[:, None]
    relative = position - offsets[None, :]
    steps = jnp.arange(width_max, dtype=jnp.int32)[:, None, None]
    picked = (relative[None, :, :] == steps) & (steps < stencil_widths[None, None, :])
    coeff_table = stencil_coeffs.T[:, None, :].astype(F32)
    weights = jnp.sum(jnp.where(picked, coeff_table, 0.0), axis=0).astype(BF16)
    resampled = jnp.dot(extended, weights, preferred_element_type=F32).astype(BF16)
    scale = 1.0 / (rows * lax.axis_size("space"))
    share = rows // lax.axis_size("tm")
    whole = lax.all_gather(resampled, "tm", axis=1, tiled=True)
    partial_value = lax.dot_general(
        resampled, whole, (((0,), (0,)), ((), ())), preferred_element_type=F32
    )
    every_panel = lax.all_gather(panels, "tm", axis=0, tiled=True)
    mine = lax.dynamic_slice_in_dim(whole, lax.axis_index("tm") * share, share, 0)
    modes = jnp.dot(mine, every_panel, preferred_element_type=F32).astype(BF16)
    partial_value = partial_value * scale
    gram = lax.psum_scatter(partial_value, "space", scatter_dimension=0, tiled=True)
    return (gram, modes)


def spread(packed, width_max, block):
    table = packed.astype(F32)
    rows = table.shape[0]
    moved = table[width_max : width_max + 1, :].astype(jnp.int32)
    index = lax.broadcasted_iota(jnp.int32, table.shape, 0)
    value = jnp.where(index < width_max, table, 0.0)
    step = 1
    while step < block:
        chosen = (moved & step) != 0
        if step < 8:
            other = pltpu.roll(value, step, 0)
        else:
            empty = jnp.zeros((step, block), F32)
            other = jnp.concatenate([empty, value], axis=0)
            value = jnp.concatenate([value, empty], axis=0)
        value = jnp.where(jnp.broadcast_to(chosen, value.shape), other, value)
        step *= 2
    return value


def kernel(
    nsp, ntm, chunks, halves, width_max,
    snap, starts_in, widths_in, coeffs_in, panels,
    gram_out, modes_out,
    starts, widths, coeffs,
    packed, weights, gathered, resampled, acc, pair_in, mine32, tm_out, tm_in, z_out, z_in, panel_all,
    local_sem, pack_send, pack_recv, row_send, row_recv, panel_send, panel_recv, relay_send, relay_recv,
    pair_send, pair_recv, tm_send, tm_recv, z_send, z_recv,
):
    space = lax.axis_index("space")
    t = lax.axis_index("tm")
    zz, core = space // CORES, space % CORES
    nz = nsp // CORES
    block = snap.shape[1]
    share = snap.shape[0] // ntm
    piece = share // chunks
    nu = block * ntm
    wide = nu // halves

    def at(space_id, tm_id):
        return dict(device_id=(space_id, tm_id), device_id_type=pl.DeviceIdType.MESH)

    tm_peers = [t ^ mask for mask in range(ntm - 1, 0, -1)]
    z_peers = [lax.rem(zz + d, nz) * CORES + core for d in range(1, nz)]
    partner = zz * CORES + (1 - core)

    half = block // CORES

    def share_of(tm_id, core_id=core):
        return pl.ds(pl.multiple_of(tm_id * block + core_id * half, half), half)

    barrier = pltpu.get_barrier_semaphore()
    for peer in z_peers:
        pl.semaphore_signal(barrier, inc=1, **at(peer, t))
    for peer in tm_peers:
        pl.semaphore_signal(barrier, inc=1, **at(space, peer))
    pl.semaphore_signal(barrier, inc=1, **at(partner, t))

    columns = pl.ds(pl.multiple_of(t * block, block), block)
    small = [
        pltpu.make_async_copy(source, target, local_sem.at[i])
        for i, (source, target) in enumerate(
            [(starts_in, starts), (widths_in, widths), (coeffs_in, coeffs)]
        )
    ]
    own_rows = pltpu.make_async_copy(
        snap.at[pl.ds(pl.multiple_of(t * share, share), share), :], gathered.at[:, columns], local_sem.at[3]
    )
    own_panels = pltpu.make_async_copy(panels, panel_all.at[columns, :], local_sem.at[4])
    for copy in small:
        copy.start()
    own_rows.start()
    own_panels.start()

    for copy in small:
        copy.wait()
    prow = packed.shape[1]
    turned = jnp.concatenate(
        [coeffs[...].astype(F32), jnp.zeros((prow - width_max, block), F32)], axis=0
    )
    index = lax.broadcasted_iota(jnp.int32, turned.shape, 0)
    offset = (starts[...] - t * block).astype(F32)
    table = jnp.where(index < jnp.broadcast_to(widths[...], turned.shape), turned, 0.0)
    table = jnp.where(index == width_max, jnp.broadcast_to(offset, turned.shape), table)
    packed[t] = table.astype(BF16)

    pl.semaphore_wait(barrier, len(z_peers) + len(tm_peers) + 1)

    sends = []

    def send(src, dst, send_sem, recv_sem, space_id, tm_id):
        copy = pltpu.make_async_remote_copy(
            src_ref=src, dst_ref=dst, send_sem=send_sem, recv_sem=recv_sem, **at(space_id, tm_id))
        copy.start()
        sends.append(copy)

    for i, peer in enumerate(tm_peers):
        send(packed.at[t], packed.at[t], pack_send.at[i], pack_recv.at[i], space, peer)
    for c in range(chunks):
        for i, peer in enumerate(tm_peers):
            send(
                snap.at[pl.ds(pl.multiple_of(peer * share + c * piece, piece), piece), :],
                gathered.at[pl.ds(c * piece, piece), columns],
                row_send.at[c, i], row_recv.at[c, i], space, peer)
    for i, peer in enumerate(tm_peers):
        send(
            panels.at[pl.ds(pl.multiple_of(core * half, half), half), :], panel_all.at[share_of(t), :],
            panel_send.at[i], panel_recv.at[i], space, peer)

    weights[...] = jnp.zeros_like(weights)
    acc[...] = jnp.zeros_like(acc)

    def arrived(dst, sem):
        pltpu.make_async_remote_copy(
            src_ref=dst, dst_ref=dst, send_sem=sem, recv_sem=sem, **at(space, tm_peers[0])
        ).wait_recv()

    for i, origin in enumerate(tm_peers):
        arrived(packed.at[origin], pack_recv.at[i])
    for b in range(ntm):
        value = spread(packed[b], width_max, block).astype(BF16)
        height = min(value.shape[0], nu - b * block)
        weights[b * block : b * block + height, b * block : (b + 1) * block] = value[:height]

    own_rows.wait()
    span = CORES * block

    def resample(c):
        at_rows = pl.ds(pl.multiple_of(c * piece, piece), piece)
        for i, origin in enumerate(tm_peers):
            arrived(
                gathered.at[at_rows, pl.ds(pl.multiple_of(origin * block, block), block)], row_recv.at[c, i]
            )
        for first in range(0, nu, span):
            last = min(first + 2 * span, nu)
            part = jnp.dot(
                gathered[at_rows, first:last], weights[first:last, first : first + span],
                preferred_element_type=F32,
            )
            resampled[at_rows, first : first + span] = part.astype(BF16)
        return resampled[at_rows, :]

    def product(left, right):
        value = lax.dot_general(left, right, (((0,), (0,)), ((), ())), preferred_element_type=F32)
        return value.reshape(acc.shape[:3] + (right.shape[1],))

    def chunk_step(c, carry):
        rows = resample(c)
        acc[...] += product(rows, rows)
        return carry

    lax.fori_loop(0, chunks - 1, chunk_step, 0)
    parts = [slice(h * wide, (h + 1) * wide) for h in range(halves)]
    rows = resample(chunks - 1)
    for h, part in enumerate(parts):
        acc[:, :, :, part] += product(rows, rows[:, part])
        send(acc.at[:, 1 - core, :, part], pair_in.at[:, :, part], pair_send.at[h], pair_recv.at[h], partner, t)

    for h, part in enumerate(parts):
        arrived(pair_in.at[:, :, part], pair_recv.at[h])
        summed = acc[:, pl.ds(core, 1), :, part].reshape(pair_in.shape[:2] + (wide,)) + pair_in[:, :, part]
        summed = summed.reshape(mine32.shape[:3] + (wide,))
        mine32[:, :, :, part] = summed
        tm_out[:, :, :, part] = summed.astype(BF16)
        for i, peer in enumerate(tm_peers):
            send(
                tm_out.at[peer, :, :, part], tm_in.at[i, :, :, part],
                tm_send.at[h, i], tm_recv.at[h, i], space, peer)

    for i, origin in enumerate(tm_peers):
        arrived(panel_all.at[share_of(origin), :], panel_recv.at[i])
        send(
            panel_all.at[share_of(origin), :], panel_all.at[share_of(origin), :],
            relay_send.at[i], relay_recv.at[i], partner, t)

    for h, part in enumerate(parts):
        total = mine32[pl.ds(t, 1), :, :, part].reshape(z_out.shape[:2] + (wide,))
        for i in range(ntm - 1):
            arrived(tm_in.at[i, :, :, part], tm_recv.at[h, i])
            total = total + tm_in[i, :, :, part].astype(F32)
        mine32[pl.ds(t, 1), :, :, part] = total[None]
        z_out[:, :, part] = total.astype(BF16)
        for i, peer in enumerate(z_peers):
            send(
                z_out.at[lax.rem(zz + i + 1, nz), :, part], z_in.at[i, :, part],
                z_send.at[h, i], z_recv.at[h, i], peer, t)
    own_panels.wait()
    for i, origin in enumerate(tm_peers):
        arrived(panel_all.at[share_of(origin, 1 - core), :], relay_recv.at[i])

    def modes_step(c, carry):
        at_rows = pl.ds(pl.multiple_of(c * piece, piece), piece)
        modes_out[at_rows, :] = jnp.dot(
            resampled[at_rows, :], panel_all[...], preferred_element_type=F32).astype(BF16)
        return carry

    lax.fori_loop(0, chunks, modes_step, 0)

    for h, part in enumerate(parts):
        final = mine32[pl.ds(t, 1), pl.ds(zz, 1), :, part].reshape(gram_out.shape[0], wide)
        for i in range(nz - 1):
            arrived(z_in.at[i, :, part], z_recv.at[h, i])
            final = final + z_in[i, :, part].astype(F32)
        gram_out[:, part] = final * (1.0 / (snap.shape[0] * nsp))

    for copy in sends:
        copy.wait_send()


def fused(nsp, ntm, snapshots, stencil_starts, stencil_widths, stencil_coeffs, panels):
    rows, block = snapshots.shape
    width_max = stencil_coeffs.shape[1]
    nmode = panels.shape[1]
    nu, share, nz = block * ntm, rows // ntm, nsp // CORES
    own = nu // (ntm * nsp)
    chunks, halves = CHUNKS, 2
    prow = -(-(width_max + 1) // 16) * 16
    vmem = pl.BlockSpec(memory_space=pltpu.VMEM)
    hbm = pl.BlockSpec(memory_space=pltpu.HBM)
    dma = pltpu.SemaphoreType.DMA
    call = pl.pallas_call(
        functools.partial(kernel, nsp, ntm, chunks, halves, width_max),
        out_shape=(
            jax.ShapeDtypeStruct((own, nu), F32),
            jax.ShapeDtypeStruct((share, nmode), BF16),
        ),
        in_specs=[hbm, hbm, hbm, hbm, hbm],
        out_specs=(vmem, vmem),
        scratch_shapes=[
            pltpu.VMEM((1, block), jnp.int32),
            pltpu.VMEM((1, block), jnp.int32),
            pltpu.VMEM((width_max, block), BF16),
            pltpu.VMEM((ntm, prow, block), BF16),
            pltpu.VMEM((nu, nu), BF16),
            pltpu.VMEM((share, nu), BF16),
            pltpu.VMEM((share, nu), BF16),
            pltpu.VMEM((ntm * nz, CORES, own, nu), F32),
            pltpu.VMEM((ntm * nz, own, nu), F32),
            pltpu.VMEM((ntm, nz, own, nu), F32),
            pltpu.VMEM((ntm, nz, own, nu), BF16),
            pltpu.VMEM((ntm - 1, nz, own, nu), BF16),
            pltpu.VMEM((nz, own, nu), BF16),
            pltpu.VMEM((nz - 1, own, nu), BF16),
            pltpu.VMEM((nu, nmode), BF16),
            dma((5,)),
            dma((ntm - 1,)),
            dma((ntm - 1,)),
            dma((chunks, ntm - 1)),
            dma((chunks, ntm - 1)),
            dma((ntm - 1,)),
            dma((ntm - 1,)),
            dma((ntm - 1,)),
            dma((ntm - 1,)),
            dma((halves,)),
            dma((halves,)),
            dma((halves, ntm - 1)),
            dma((halves, ntm - 1)),
            dma((halves, nz - 1)),
            dma((halves, nz - 1)),
        ],
        compiler_params=pltpu.CompilerParams(
            collective_id=0, has_side_effects=True, vmem_limit_bytes=48 * 1024 * 1024
        ),
    )
    operands = (
        snapshots, stencil_starts.reshape(1, block), stencil_widths.reshape(1, block), stencil_coeffs.T, panels
    )
    values = call(*(pltpu.with_memory_space_constraint(operand, pltpu.HBM) for operand in operands))
    return pl.pallas_call(
        store,
        out_shape=tuple(jax.ShapeDtypeStruct(value.shape, value.dtype) for value in values),
        in_specs=[vmem, vmem],
        out_specs=(hbm, hbm),
        scratch_shapes=[dma((2,))],
    )(*(pltpu.with_memory_space_constraint(value, pltpu.VMEM) for value in values))


def store(gram, modes, gram_out, modes_out, sem):
    copies = [
        pltpu.make_async_copy(modes, modes_out, sem.at[0]),
        pltpu.make_async_copy(gram, gram_out, sem.at[1]),
    ]
    for copy in copies:
        copy.start()
    for copy in copies:
        copy.wait()


def solution(mesh):
    nsp, ntm = mesh.shape["space"], mesh.shape["tm"]

    def body(snapshots, stencil_starts, stencil_widths, stencil_coeffs, panels):
        rows, block = snapshots.shape
        own = block // nsp
        fits = block == 128 and own % 16 == 0 and nsp % CORES == 0 and ntm % 2 == 0 and ntm & (ntm - 1) == 0 and rows % (64 * ntm) == 0
        if fits and 4 * (block * ntm) ** 2 <= 4 * 1024 * 1024:
            return fused(nsp, ntm, snapshots, stencil_starts, stencil_widths, stencil_coeffs, panels)
        return on_device(snapshots, stencil_starts, stencil_widths, stencil_coeffs, panels)

    return jax.shard_map(
        body,
        mesh=mesh,
        in_specs=(P("space", "tm"), P("tm"), P("tm"), P("tm", None), P("tm", None)),
        out_specs=(P(("tm", "space"), None), P(("space", "tm"), None)),
        check_vma=False,
    )
```

```python
import functools

import jax
import jax.numpy as jnp
from jax import lax
from jax.experimental import pallas as pl
from jax.experimental.pallas import tpu as pltpu
from jax.sharding import PartitionSpec as P

F32 = jnp.float32
BF16 = jnp.bfloat16
CORES = 2
CHUNKS = 8


def shifted(value, axis, steps):
    count = lax.axis_size(axis)
    initial, last = (max(0, -steps), min(count, count - steps))
    return lax.ppermute(value, axis, [(source, source + steps) for source in range(initial, last)])


def on_device(snapshots, stencil_starts, stencil_widths, stencil_coeffs, panels):
    rows, block = snapshots.shape
    width_max = stencil_coeffs.shape[1]
    rim = shifted(snapshots[:, : width_max - 1], "tm", -1)
    extended = jnp.concatenate([snapshots, rim], axis=1)
    offsets = stencil_starts - lax.axis_index("tm") * block
    position = jnp.arange(block + width_max - 1, dtype=jnp.int32)[:, None]
    relative = position - offsets[None, :]
    steps = jnp.arange(width_max, dtype=jnp.int32)[:, None, None]
    picked = (relative[None, :, :] == steps) & (steps < stencil_widths[None, None, :])
    coeff_table = stencil_coeffs.T[:, None, :].astype(F32)
    weights = jnp.sum(jnp.where(picked, coeff_table, 0.0), axis=0).astype(BF16)
    resampled = jnp.dot(extended, weights, preferred_element_type=F32).astype(BF16)
    scale = 1.0 / (rows * lax.axis_size("space"))
    share = rows // lax.axis_size("tm")
    whole = lax.all_gather(resampled, "tm", axis=1, tiled=True)
    partial_value = lax.dot_general(
        resampled, whole, (((0,), (0,)), ((), ())), preferred_element_type=F32
    )
    every_panel = lax.all_gather(panels, "tm", axis=0, tiled=True)
    mine = lax.dynamic_slice_in_dim(whole, lax.axis_index("tm") * share, share, 0)
    modes = jnp.dot(mine, every_panel, preferred_element_type=F32).astype(BF16)
    partial_value = partial_value * scale
    gram = lax.psum_scatter(partial_value, "space", scatter_dimension=0, tiled=True)
    return (gram, modes)


def spread(packed, width_max, block):
    table = packed.astype(F32)
    rows = table.shape[0]
    moved = table[width_max : width_max + 1, :].astype(jnp.int32)
    index = lax.broadcasted_iota(jnp.int32, table.shape, 0)
    value = jnp.where(index < width_max, table, 0.0)
    step = 1
    while step < block:
        chosen = (moved & step) != 0
        if step < 8:
            other = pltpu.roll(value, step, 0)
        else:
            empty = jnp.zeros((step, block), F32)
            other = jnp.concatenate([empty, value], axis=0)
            value = jnp.concatenate([value, empty], axis=0)
        value = jnp.where(jnp.broadcast_to(chosen, value.shape), other, value)
        step *= 2
    return value


def kernel(
    nsp, ntm, chunks, halves, width_max,
    snap, starts_in, widths_in, coeffs_in, panels,
    gram_out, modes_out,
    starts, widths, coeffs,
    packed, weights, gathered, resampled, acc, pair_in, mine32, tm_out, tm_in, z_out, z_in, panel_all,
    local_sem, pack_send, pack_recv, row_send, row_recv, panel_send, panel_recv, relay_send, relay_recv, hand_send, hand_recv,
    pair_send, pair_recv, tm_send, tm_recv, z_send, z_recv,
):
    space = lax.axis_index("space")
    t = lax.axis_index("tm")
    zz, core = space // CORES, space % CORES
    nz = nsp // CORES
    block = snap.shape[1]
    share = snap.shape[0] // ntm
    piece = share // chunks
    nu = block * ntm
    wide = nu // halves

    def at(space_id, tm_id):
        return dict(device_id=(space_id, tm_id), device_id_type=pl.DeviceIdType.MESH)

    tm_peers = [t ^ mask for mask in range(ntm - 1, 0, -1)]
    z_peers = [lax.rem(zz + d, nz) * CORES + core for d in range(1, nz)]
    partner = zz * CORES + (1 - core)

    half = block // CORES

    def share_of(tm_id, core_id=core):
        return pl.ds(pl.multiple_of(tm_id * block + core_id * half, half), half)

    def table_of(tm_id, core_id=core):
        rows = packed.shape[1] // CORES
        return packed.at[tm_id, pl.ds(pl.multiple_of(core_id * rows, rows), rows), :]

    barrier = pltpu.get_barrier_semaphore()
    for peer in z_peers:
        pl.semaphore_signal(barrier, inc=1, **at(peer, t))
    for peer in tm_peers:
        pl.semaphore_signal(barrier, inc=1, **at(space, peer))
    pl.semaphore_signal(barrier, inc=1, **at(partner, t))

    columns = pl.ds(pl.multiple_of(t * block, block), block)
    small = [
        pltpu.make_async_copy(source, target, local_sem.at[i])
        for i, (source, target) in enumerate(
            [(starts_in, starts), (widths_in, widths), (coeffs_in, coeffs)]
        )
    ]
    own_rows = pltpu.make_async_copy(
        snap.at[pl.ds(pl.multiple_of(t * share, share), share), :], gathered.at[:, columns], local_sem.at[3]
    )
    own_panels = pltpu.make_async_copy(panels, panel_all.at[columns, :], local_sem.at[4])
    for copy in small:
        copy.start()
    own_rows.start()
    own_panels.start()

    for copy in small:
        copy.wait()
    prow = packed.shape[1]
    turned = jnp.concatenate(
        [coeffs[...].astype(F32), jnp.zeros((prow - width_max, block), F32)], axis=0
    )
    index = lax.broadcasted_iota(jnp.int32, turned.shape, 0)
    offset = (starts[...] - t * block).astype(F32)
    table = jnp.where(index < jnp.broadcast_to(widths[...], turned.shape), turned, 0.0)
    table = jnp.where(index == width_max, jnp.broadcast_to(offset, turned.shape), table)
    packed[t] = table.astype(BF16)

    pl.semaphore_wait(barrier, len(z_peers) + len(tm_peers) + 1)

    sends = []

    def send(src, dst, send_sem, recv_sem, space_id, tm_id):
        copy = pltpu.make_async_remote_copy(
            src_ref=src, dst_ref=dst, send_sem=send_sem, recv_sem=recv_sem, **at(space_id, tm_id))
        copy.start()
        sends.append(copy)

    for i, peer in enumerate(tm_peers):
        send(table_of(t), table_of(t), pack_send.at[i], pack_recv.at[i], space, peer)
    for c in range(chunks):
        for i, peer in enumerate(tm_peers):
            send(
                snap.at[pl.ds(pl.multiple_of(peer * share + c * piece, piece), piece), :],
                gathered.at[pl.ds(c * piece, piece), columns],
                row_send.at[c, i], row_recv.at[c, i], space, peer)
    for i, peer in enumerate(tm_peers):
        send(
            panels.at[pl.ds(pl.multiple_of(core * half, half), half), :], panel_all.at[share_of(t), :],
            panel_send.at[i], panel_recv.at[i], space, peer)

    weights[...] = jnp.zeros_like(weights)
    acc[...] = jnp.zeros_like(acc)

    def arrived(dst, sem):
        pltpu.make_async_remote_copy(
            src_ref=dst, dst_ref=dst, send_sem=sem, recv_sem=sem, **at(space, tm_peers[0])
        ).wait_recv()

    for i, origin in enumerate(tm_peers):
        arrived(table_of(origin), pack_recv.at[i])
        send(table_of(origin), table_of(origin), hand_send.at[i], hand_recv.at[i], partner, t)
    for i, origin in enumerate(tm_peers):
        arrived(table_of(origin, 1 - core), hand_recv.at[i])
    for b in range(ntm):
        value = spread(packed[b], width_max, block).astype(BF16)
        height = min(value.shape[0], nu - b * block)
        weights[b * block : b * block + height, b * block : (b + 1) * block] = value[:height]

    own_rows.wait()
    span = CORES * block

    def resample(c):
        at_rows = pl.ds(pl.multiple_of(c * piece, piece), piece)
        for i, origin in enumerate(tm_peers):
            arrived(
                gathered.at[at_rows, pl.ds(pl.multiple_of(origin * block, block), block)], row_recv.at[c, i]
            )
        for first in range(0, nu, span):
            last = min(first + 2 * span, nu)
            part = jnp.dot(
                gathered[at_rows, first:last], weights[first:last, first : first + span],
                preferred_element_type=F32,
            )
            resampled[at_rows, first : first + span] = part.astype(BF16)
        return resampled[at_rows, :]

    def product(left, right):
        value = lax.dot_general(left, right, (((0,), (0,)), ((), ())), preferred_element_type=F32)
        return value.reshape(acc.shape[:3] + (right.shape[1],))

    def chunk_step(c, carry):
        rows = resample(c)
        acc[...] += product(rows, rows)
        return carry

    lax.fori_loop(0, chunks - 1, chunk_step, 0)
    parts = [slice(h * wide, (h + 1) * wide) for h in range(halves)]
    rows = resample(chunks - 1)
    for h, part in enumerate(parts):
        acc[:, :, :, part] += product(rows, rows[:, part])
        send(acc.at[:, 1 - core, :, part], pair_in.at[:, :, part], pair_send.at[h], pair_recv.at[h], partner, t)

    for h, part in enumerate(parts):
        arrived(pair_in.at[:, :, part], pair_recv.at[h])
        summed = acc[:, pl.ds(core, 1), :, part].reshape(pair_in.shape[:2] + (wide,)) + pair_in[:, :, part]
        summed = summed.reshape(mine32.shape[:3] + (wide,))
        mine32[:, :, :, part] = summed
        tm_out[:, :, :, part] = summed.astype(BF16)
        for i, peer in enumerate(tm_peers):
            send(
                tm_out.at[peer, :, :, part], tm_in.at[i, :, :, part],
                tm_send.at[h, i], tm_recv.at[h, i], space, peer)

    for i, origin in enumerate(tm_peers):
        arrived(panel_all.at[share_of(origin), :], panel_recv.at[i])
        send(
            panel_all.at[share_of(origin), :], panel_all.at[share_of(origin), :],
            relay_send.at[i], relay_recv.at[i], partner, t)

    for h, part in enumerate(parts):
        total = mine32[pl.ds(t, 1), :, :, part].reshape(z_out.shape[:2] + (wide,))
        for i in range(ntm - 1):
            arrived(tm_in.at[i, :, :, part], tm_recv.at[h, i])
            total = total + tm_in[i, :, :, part].astype(F32)
        mine32[pl.ds(t, 1), :, :, part] = total[None]
        z_out[:, :, part] = total.astype(BF16)
        for i, peer in enumerate(z_peers):
            send(
                z_out.at[lax.rem(zz + i + 1, nz), :, part], z_in.at[i, :, part],
                z_send.at[h, i], z_recv.at[h, i], peer, t)
    own_panels.wait()
    for i, origin in enumerate(tm_peers):
        arrived(panel_all.at[share_of(origin, 1 - core), :], relay_recv.at[i])

    def modes_step(c, carry):
        at_rows = pl.ds(pl.multiple_of(c * piece, piece), piece)
        modes_out[at_rows, :] = jnp.dot(
            resampled[at_rows, :], panel_all[...], preferred_element_type=F32).astype(BF16)
        return carry

    lax.fori_loop(0, chunks, modes_step, 0)

    for h, part in enumerate(parts):
        final = mine32[pl.ds(t, 1), pl.ds(zz, 1), :, part].reshape(gram_out.shape[0], wide)
        for i in range(nz - 1):
            arrived(z_in.at[i, :, part], z_recv.at[h, i])
            final = final + z_in[i, :, part].astype(F32)
        gram_out[:, part] = final * (1.0 / (snap.shape[0] * nsp))

    for copy in sends:
        copy.wait_send()


def fused(nsp, ntm, snapshots, stencil_starts, stencil_widths, stencil_coeffs, panels):
    rows, block = snapshots.shape
    width_max = stencil_coeffs.shape[1]
    nmode = panels.shape[1]
    nu, share, nz = block * ntm, rows // ntm, nsp // CORES
    own = nu // (ntm * nsp)
    chunks, halves = CHUNKS, 2
    prow = -(-(width_max + 1) // 32) * 32
    vmem = pl.BlockSpec(memory_space=pltpu.VMEM)
    hbm = pl.BlockSpec(memory_space=pltpu.HBM)
    dma = pltpu.SemaphoreType.DMA
    call = pl.pallas_call(
        functools.partial(kernel, nsp, ntm, chunks, halves, width_max),
        out_shape=(
            jax.ShapeDtypeStruct((own, nu), F32),
            jax.ShapeDtypeStruct((share, nmode), BF16),
        ),
        in_specs=[hbm, hbm, hbm, hbm, hbm],
        out_specs=(vmem, vmem),
        scratch_shapes=[
            pltpu.VMEM((1, block), jnp.int32),
            pltpu.VMEM((1, block), jnp.int32),
            pltpu.VMEM((width_max, block), BF16),
            pltpu.VMEM((ntm, prow, block), BF16),
            pltpu.VMEM((nu, nu), BF16),
            pltpu.VMEM((share, nu), BF16),
            pltpu.VMEM((share, nu), BF16),
            pltpu.VMEM((ntm * nz, CORES, own, nu), F32),
            pltpu.VMEM((ntm * nz, own, nu), F32),
            pltpu.VMEM((ntm, nz, own, nu), F32),
            pltpu.VMEM((ntm, nz, own, nu), BF16),
            pltpu.VMEM((ntm - 1, nz, own, nu), BF16),
            pltpu.VMEM((nz, own, nu), BF16),
            pltpu.VMEM((nz - 1, own, nu), BF16),
            pltpu.VMEM((nu, nmode), BF16),
            dma((5,)),
            dma((ntm - 1,)),
            dma((ntm - 1,)),
            dma((chunks, ntm - 1)),
            dma((chunks, ntm - 1)),
            dma((ntm - 1,)),
            dma((ntm - 1,)),
            dma((ntm - 1,)),
            dma((ntm - 1,)),
            dma((ntm - 1,)),
            dma((ntm - 1,)),
            dma((halves,)),
            dma((halves,)),
            dma((halves, ntm - 1)),
            dma((halves, ntm - 1)),
            dma((halves, nz - 1)),
            dma((halves, nz - 1)),
        ],
        compiler_params=pltpu.CompilerParams(
            collective_id=0, has_side_effects=True, vmem_limit_bytes=48 * 1024 * 1024
        ),
    )
    operands = (
        snapshots, stencil_starts.reshape(1, block), stencil_widths.reshape(1, block), stencil_coeffs.T, panels
    )
    values = call(*(pltpu.with_memory_space_constraint(operand, pltpu.HBM) for operand in operands))
    return pl.pallas_call(
        store,
        out_shape=tuple(jax.ShapeDtypeStruct(value.shape, value.dtype) for value in values),
        in_specs=[vmem, vmem],
        out_specs=(hbm, hbm),
        scratch_shapes=[dma((2,))],
    )(*(pltpu.with_memory_space_constraint(value, pltpu.VMEM) for value in values))


def store(gram, modes, gram_out, modes_out, sem):
    copies = [
        pltpu.make_async_copy(modes, modes_out, sem.at[0]),
        pltpu.make_async_copy(gram, gram_out, sem.at[1]),
    ]
    for copy in copies:
        copy.start()
    for copy in copies:
        copy.wait()


def solution(mesh):
    nsp, ntm = mesh.shape["space"], mesh.shape["tm"]

    def body(snapshots, stencil_starts, stencil_widths, stencil_coeffs, panels):
        rows, block = snapshots.shape
        own = block // nsp
        fits = block == 128 and own % 16 == 0 and nsp % CORES == 0 and ntm % 2 == 0 and ntm & (ntm - 1) == 0 and rows % (64 * ntm) == 0
        if fits and 4 * (block * ntm) ** 2 <= 4 * 1024 * 1024:
            return fused(nsp, ntm, snapshots, stencil_starts, stencil_widths, stencil_coeffs, panels)
        return on_device(snapshots, stencil_starts, stencil_widths, stencil_coeffs, panels)

    return jax.shard_map(
        body,
        mesh=mesh,
        in_specs=(P("space", "tm"), P("tm"), P("tm"), P("tm", None), P("tm", None)),
        out_specs=(P(("tm", "space"), None), P(("space", "tm"), None)),
        check_vma=False,
    )
```
